256 devices in a mesh: sector: 8 (over x, core), op: 32 (over z, y).
Axes of the slice: x: 4, y: 4, z: 8, core: 2. Of those that a mesh axis runs over, the one named last changes fastest.
Arguments:
- wavefunction: bfloat16 [16, 512, 512], P('sector', 'op'), may hold values from -6 to 6
- sector_bases: bfloat16 [16, 512, 512], P('sector', 'op'), may hold values from -1 to 1
- left_env: bfloat16 [1536, 512, 512], P(('sector', 'op')), may hold values from -0.25 to 0.25
- right_env: bfloat16 [1536, 512, 512], P(('sector', 'op')), may hold values from -0.02734375 to 0.02734375
- pair_source: int32 [1536], P(('sector', 'op')), may hold values from 0 to 15, as said below
- pair_target: int32 [1536], P(('sector', 'op')), may hold values from 0 to 15
- sector_slot: int32 [16], replicated, may hold values from 0 to 15, as said below
- orders: int32 [16], replicated, may hold values from 256 to 512, as said below
Outputs:
- sigma_blocks: bfloat16 [16, 512, 512], P('sector', 'op')
- left_rotated: bfloat16 [1536, 512, 512], P(('sector', 'op'))
The draws below stay inside these ranges and needn't reach their ends.
Inputs may be any that keep to these rules, and one draw needn't show every extreme that they name: A permutation: sector s's blocks stand at slot sector_slot[s]. `pair_source`: the pairs held by index i of the sector axis have sources whose slots lie in i * 2 to (i + 1) * 2 - 1. `orders`: some sector has order exactly 512.
All inputs are finite; a program needn't handle non-finite values.
Results may differ from the reference program's by a relative error of at most 0.0049.
Values may be sent and summed in bfloat16 or wider, within the bound.
No kernel may reach another device: no remote copies, remote signals or barrier semaphores. Data moves between devices by JAX's collectives and lax.ppermute only.
A program may use at most 128 MiB of HBM per device.

```python
import jax
import jax.numpy as jnp
from jax import lax

K = 512
SEC_DEV = 2
PAIRS_DEV = 6
SECTORS = 16
PAIRS = 1536
N_SECTOR = 8
N_OP = 32


def slot_table(key):
    return jax.random.permutation(jax.random.fold_in(key, 11), SECTORS).astype(jnp.int32)


def draw_sector_slot(key, part):
    return slot_table(key)


def draw_pair_source(key, part):
    table = slot_table(key)
    sector_of = jnp.argsort(table, stable=True).astype(jnp.int32)
    numbers = jnp.arange(PAIRS, dtype=jnp.int32)
    owner_ids = numbers // (PAIRS // N_SECTOR)
    picks = jax.random.randint(jax.random.fold_in(key, 12), (PAIRS,), 0, SEC_DEV, dtype=jnp.int32)
    return sector_of[owner_ids * SEC_DEV + picks]


def draw_orders(key, part):
    base = jax.random.randint(jax.random.fold_in(key, 14), (SECTORS,), K // 2, K + 1, dtype=jnp.int32)
    marked = jax.random.randint(jax.random.fold_in(key, 15), (), 0, SECTORS, dtype=jnp.int32)
    labels = jnp.arange(SECTORS, dtype=jnp.int32)
    return jnp.where(labels == marked, K, base).astype(jnp.int32)


def plant(drawn, rng, low, largest):
    index_at = [jax.random.randint(jax.random.fold_in(rng, axis), (), 0, length) for axis, length in enumerate(drawn.shape)]
    main_axis = drawn.shape.index(max(drawn.shape))
    neighbour = index_at[:main_axis] + [(index_at[main_axis] + 1) % drawn.shape[main_axis]] + index_at[main_axis + 1:]
    return drawn.at[tuple(index_at)].set(low).at[tuple(neighbour)].set(largest)


def steps_of(stream_key, shape, pieces, low, top_value):
    def one(position, parts):
        heights = jax.random.uniform(jax.random.fold_in(jax.random.fold_in(stream_key, 6), position), (parts,), jnp.float32, low / len(pieces), top_value / len(pieces))
        return jnp.repeat(jnp.exp(heights), shape[position] // parts).reshape((-1,) + (1,) * (len(shape) - position - 1))

    gain = one(*pieces[0])
    for cut in pieces[1:]:
        gain = gain * one(*cut)
    return gain


def gaussian(key, shape, spread, limit, pieces=(), kind=jnp.bfloat16):
    loudness = steps_of(key, shape, pieces, -0.22, 0.18) if pieces else 1.0
    values = jax.random.normal(key, shape, jnp.float32) * spread * loudness
    return jnp.minimum(jnp.maximum(values, -limit), limit).astype(kind)


def setup_inputs(seed: int = 0) -> dict:
    seeds = jax.random.split(jax.random.key(seed), 9)
    return {
        "wavefunction": gaussian(seeds[0], (SECTORS, K, K), 1.0, 6.0, ((0, 8), (1, 32))),
        "sector_bases": gaussian(seeds[1], (SECTORS, K, K), (K // 16) ** -0.5, 1.0, ((0, 8), (1, 32))),
        "left_env": gaussian(seeds[2], (PAIRS, K, K), K ** -0.5, 0.25, ((0, 256),)),
        "right_env": gaussian(seeds[3], (PAIRS, K, K), (K * PAIRS_DEV * N_OP // SEC_DEV) ** -0.5, 0.02734375, ((0, 256),)),
        "pair_source": draw_pair_source(jax.random.fold_in(seeds[8], 71), 0),
        "pair_target": plant(jax.random.randint(seeds[5], (PAIRS,), 0, SECTORS), jax.random.fold_in(seeds[5], 1), 0, SECTORS - 1).astype(jnp.int32),
        "sector_slot": draw_sector_slot(jax.random.fold_in(seeds[8], 71), 0),
        "orders": draw_orders(jax.random.fold_in(seeds[8], 71), 0),
    }


def reference(wavefunction, sector_bases, left_env, right_env, pair_source, pair_target, sector_slot, orders):
    sectors = orders.shape[0]
    width = wavefunction.shape[1]
    slot_order = jnp.zeros((sectors,), jnp.int32).at[sector_slot].set(orders)
    positions = jnp.arange(width, dtype=jnp.int32)
    edge = positions[None, :] < slot_order[:, None]
    inside = edge[:, :, None] & edge[:, None, :]
    masked = jnp.where(inside, wavefunction, jnp.zeros((), wavefunction.dtype))
    source_slot = sector_slot[pair_source].astype(jnp.int32)
    target_slot = sector_slot[pair_target].astype(jnp.int32)

    def apply_pair(totals, entry):
        left_block, right_block, source_at, target_at = entry
        projected = jnp.dot(left_block, masked[source_at], preferred_element_type=jnp.float32).astype(jnp.bfloat16)
        product = jnp.dot(projected, right_block.T, preferred_element_type=jnp.float32)
        totals = totals.at[target_at].add(product)
        half_rotated = jnp.dot(left_block, sector_bases[source_at], preferred_element_type=jnp.float32).astype(jnp.bfloat16)
        rotated = jnp.dot(sector_bases[target_at].T, half_rotated, preferred_element_type=jnp.float32).astype(jnp.bfloat16)
        return totals, rotated

    start_sum = jnp.zeros((sectors, width, width), jnp.float32)
    totals, left_rotated = lax.scan(apply_pair, start_sum, (left_env, right_env, source_slot, target_slot))
    sigma_blocks = jnp.where(inside, totals, jnp.zeros((), jnp.float32)).astype(jnp.bfloat16)
    return sigma_blocks, left_rotated
```

```python
import jax
import jax.numpy as jnp
from jax import lax
from jax.experimental import pallas as pl
from jax.experimental.pallas import tpu as pltpu
from jax.sharding import PartitionSpec as P


NX, NC, NZ, NY = 4, 2, 8, 4
SLOTS = 2
SECTORS = 16
PAIRS = 6
ROWS = 16
K = 512
BF = jnp.bfloat16
F32 = jnp.float32
DIST = (1, 3, 2)


SMEM = pl.BlockSpec(memory_space=pltpu.SMEM)
ANY = pl.BlockSpec(memory_space=pl.ANY)


def shift_y(a, d):
    perm = [(z * NY + y, z * NY + (y + d) % NY) for z in range(NZ) for y in range(NY)]
    return lax.ppermute(a, "op", perm)


def shift_x(a, d):
    perm = [(x * NC + c, (x + d) % NX * NC + c) for x in range(NX) for c in range(NC)]
    return lax.ppermute(a, "sector", perm)


def swap_core(a):
    perm = [(x * NC + c, x * NC + 1 - c) for x in range(NX) for c in range(NC)]
    return lax.ppermute(a, "sector", perm)


def exchange_z(tiles):
    groups = [[z * NY + y for z in range(NZ)] for y in range(NY)]
    return lax.all_to_all(tiles, "op", 0, 0, axis_index_groups=groups, tiled=True)


def place(dev_ref):
    dev = dev_ref[0]
    x = dev // 64
    c = dev // 32 % 2
    z = dev // 4 % 8
    y = dev % 4
    return x, c, z, y


def order_of(slot, sector_slot, orders):
    found = jnp.int32(0)
    for s in range(SECTORS):
        found = jnp.where(sector_slot[s] == slot, orders[s], found)
    return found


def source_y(y, k):
    return y if k == 0 else (y + NY - DIST[k - 1]) % NY


def products_kernel(
    dev, pair_source, sector_slot, orders, w0, w1, w2, w3, left, right, o0, o1, o2, o3, wm, pb
):
    p = pl.program_id(0)
    x, c, _, y = place(dev)
    sector = x * NC + c

    @pl.when(p == 0)
    def _():
        row_in = lax.broadcasted_iota(jnp.int32, (ROWS, K), 0)
        column = lax.broadcasted_iota(jnp.int32, (ROWS, K), 1)
        for a in range(SLOTS):
            order = order_of(sector * SLOTS + a, sector_slot, orders)
            for k, w in enumerate((w0, w1, w2, w3)):
                ys = source_y(y, k)

                def body(zz, carry, w=w, a=a, ys=ys, order=order):
                    row = row_in + (zz * NY + ys) * ROWS
                    keep = (row < order) & (column < order)
                    value = w[zz, a].astype(F32)
                    wm[a, zz, ys] = jnp.where(keep, value, 0.0).astype(BF)
                    return carry

                lax.fori_loop(0, NZ, body, 0)

    a = sector_slot[pair_source[p]] - sector * SLOTS
    w = wm[a].reshape(K, K)
    projected = jnp.dot(left[0], w, preferred_element_type=F32).astype(BF)
    product = lax.dot_general(
        projected, right[0], (((1,), (1,)), ((), ())), preferred_element_type=F32
    )
    pb[...] = product.astype(BF).reshape(NZ, NY, ROWS, K)
    o0[0] = pb[:, y]
    for d, out in zip(DIST, (o1, o2, o3)):
        out[0] = pb[:, (y + d) % NY]


def products(dev, pair_source, sector_slot, orders, ws, left, right):
    whole = pl.BlockSpec((NZ, SLOTS, ROWS, K), lambda p: (0, 0, 0, 0))
    pair = pl.BlockSpec((1, K, K), lambda p: (p, 0, 0))
    out = pl.BlockSpec((1, NZ, ROWS, K), lambda p: (p, 0, 0, 0))
    return pl.pallas_call(
        products_kernel,
        grid=(PAIRS,),
        out_shape=[jax.ShapeDtypeStruct((PAIRS, NZ, ROWS, K), BF)] * 4,
        in_specs=[SMEM] * 4 + [whole] * 4 + [pair] * 2,
        out_specs=[out] * 4,
        scratch_shapes=[
            pltpu.VMEM((SLOTS, NZ, NY, ROWS, K), BF),
            pltpu.VMEM((NZ, NY, ROWS, K), BF),
        ],
        name="products",
    )(dev, pair_source, sector_slot, orders, *ws, left, right)


def join_kernel(dev, b, out):
    _, _, _, y = place(dev)
    for k in range(NY):
        ys = source_y(y, k)
        for a in range(SLOTS):
            out[a, :, ys] = b[:, k, a]


def join(dev, b):
    vm = pl.BlockSpec(memory_space=pltpu.VMEM)
    return pl.pallas_call(
        join_kernel,
        out_shape=jax.ShapeDtypeStruct((SLOTS, NZ, NY, ROWS, K), BF),
        in_specs=[SMEM, vm],
        out_specs=vm,
        name="join",
    )(dev, b)


def half_kernel(dev, pair_source, sector_slot, bases, left, out):
    p = pl.program_id(0)
    x, c, _, _ = place(dev)
    a = sector_slot[pair_source[p]] - (x * NC + c) * SLOTS
    out[0] = jnp.dot(left[0], bases[a].reshape(K, K), preferred_element_type=F32).astype(BF)


def half(dev, pair_source, sector_slot, bases, left):
    pair = pl.BlockSpec((1, K, K), lambda p: (p, 0, 0))
    whole = pl.BlockSpec((SLOTS, NZ, NY, ROWS, K), lambda p: (0, 0, 0, 0, 0))
    return pl.pallas_call(
        half_kernel,
        grid=(PAIRS,),
        out_shape=jax.ShapeDtypeStruct((PAIRS, K, K), BF),
        in_specs=[SMEM] * 3 + [whole, pair],
        out_specs=pair,
        name="half",
    )(dev, pair_source, sector_slot, bases, left)


def rotate_kernel(dev, pair_target, sector_slot, half_ref, *rest):
    tables, out, chosen, sems = rest[:8], rest[8], rest[9], rest[10]
    p = pl.program_id(0)
    x, c, _, _ = place(dev)

    @pl.when(p == 0)
    def _():
        for q in range(PAIRS):
            slot = sector_slot[pair_target[q]]
            sector = slot // SLOTS
            a = slot % SLOTS
            behind = (x + NX - sector // NC) % NX
            same = (sector % NC) == c
            for k in range(4):
                steps = 0 if k == 0 else DIST[k - 1]
                for other in range(2):
                    hit = (behind == steps) & (same if other == 0 else jnp.logical_not(same))

                    @pl.when(hit)
                    def _(k=k, other=other):
                        pltpu.make_async_copy(
                            tables[other * 4 + k].at[a], chosen.at[q], sems.at[q]
                        ).start()

    pltpu.make_async_copy(tables[0].at[0], chosen.at[p], sems.at[p]).wait()
    basis = chosen[p].reshape(K, K)
    out[0] = lax.dot_general(
        basis, half_ref[0], (((0,), (0,)), ((), ())), preferred_element_type=F32
    ).astype(BF)


def rotate(dev, pair_target, sector_slot, halves, tables):
    pair = pl.BlockSpec((1, K, K), lambda p: (p, 0, 0))
    return pl.pallas_call(
        rotate_kernel,
        grid=(PAIRS,),
        out_shape=jax.ShapeDtypeStruct((PAIRS, K, K), BF),
        in_specs=[SMEM] * 3 + [pair] + [ANY] * 8,
        out_specs=pair,
        scratch_shapes=[
            pltpu.VMEM((PAIRS, NZ, NY, ROWS, K), BF),
            pltpu.SemaphoreType.DMA((PAIRS,)),
        ],
        name="rotate",
    )(dev, pair_target, sector_slot, halves, *tables)


ZB = 2


def by_target_kernel(dev, sector_slot, t0, t1, t2, t3, g0, g1, g2, g3, mine, other, acc):
    _, c, _, _ = place(dev)
    acc[...] = jnp.zeros_like(acc)
    for t, g in zip((t0, t1, t2, t3), (g0, g1, g2, g3)):
        for p in range(PAIRS):
            slot = sector_slot[t[p]]
            acc[slot] += g[p].astype(F32)
    for j in range(8):
        base = j // 2 * 4 + j % 2
        mine[j] = acc[base + c * 2]
        other[j] = acc[base + (1 - c) * 2].astype(BF)


def by_target(dev, sector_slot, targets, gathered):
    got = pl.BlockSpec((PAIRS, ZB, ROWS, K), lambda z: (0, z, 0, 0))
    out = pl.BlockSpec((8, ZB, ROWS, K), lambda z: (0, z, 0, 0))
    return pl.pallas_call(
        by_target_kernel,
        grid=(NZ // ZB,),
        out_shape=[
            jax.ShapeDtypeStruct((8, NZ, ROWS, K), F32),
            jax.ShapeDtypeStruct((8, NZ, ROWS, K), BF),
        ],
        in_specs=[SMEM] * 6 + [got] * 4,
        out_specs=[out] * 2,
        scratch_shapes=[pltpu.VMEM((SECTORS, ZB, ROWS, K), F32)],
        name="by_target",
    )(dev, sector_slot, *targets, *gathered)


def over_cores_kernel(dev, mine, other, e0, e1, e2, e3):
    x, _, _, _ = place(dev)
    for d, out in zip((0,) + DIST, (e0, e1, e2, e3)):
        xd = (x + d) % NX
        for a in range(SLOTS):
            j = xd * SLOTS + a
            out[a] = (mine[j] + other[j].astype(F32)).astype(out.dtype)


def over_cores(dev, mine, other):
    zb = 4
    got = pl.BlockSpec((8, zb, ROWS, K), lambda z: (0, z, 0, 0))
    out = pl.BlockSpec((SLOTS, zb, ROWS, K), lambda z: (0, z, 0, 0))
    shape = (SLOTS, NZ, ROWS, K)
    return pl.pallas_call(
        over_cores_kernel,
        grid=(NZ // zb,),
        out_shape=[jax.ShapeDtypeStruct(shape, F32)] + [jax.ShapeDtypeStruct(shape, BF)] * 3,
        in_specs=[SMEM] + [got] * 2,
        out_specs=[out] * 4,
        name="over_cores",
    )(dev, mine, other)


def over_x_kernel(e0, e1, e2, e3, out):
    for a in range(SLOTS):
        total = e0[a] + e1[a].astype(F32) + e2[a].astype(F32) + e3[a].astype(F32)
        out[:, a] = total.astype(BF)


def over_x(parts):
    vm = pl.BlockSpec(memory_space=pltpu.VMEM)
    return pl.pallas_call(
        over_x_kernel,
        out_shape=jax.ShapeDtypeStruct((NZ, SLOTS, ROWS, K), BF),
        in_specs=[vm] * 4,
        out_specs=vm,
        name="over_x",
    )(*parts)


def over_z_kernel(dev, sector_slot, orders, parts, out):
    x, c, z, y = place(dev)
    row = lax.broadcasted_iota(jnp.int32, (ROWS, K), 0) + (z * NY + y) * ROWS
    column = lax.broadcasted_iota(jnp.int32, (ROWS, K), 1)
    for a in range(SLOTS):
        order = order_of((x * NC + c) * SLOTS + a, sector_slot, orders)
        total = parts[0, a].astype(F32)
        for k in range(1, NZ):
            total = total + parts[k, a].astype(F32)
        keep = (row < order) & (column < order)
        out[a] = jnp.where(keep, total, 0.0).astype(BF)


def over_z(dev, sector_slot, orders, parts):
    vm = pl.BlockSpec(memory_space=pltpu.VMEM)
    return pl.pallas_call(
        over_z_kernel,
        out_shape=jax.ShapeDtypeStruct((SLOTS, ROWS, K), BF),
        in_specs=[SMEM] * 3 + [vm],
        out_specs=vm,
        name="over_z",
    )(dev, sector_slot, orders, parts)


def spread_z(a):
    return exchange_z(jnp.broadcast_to(a, (NZ, *a.shape)))


def per_device(
    wavefunction, sector_bases, left_env, right_env, pair_source, pair_target, sector_slot, orders
):
    dev = (lax.axis_index("sector") * (NZ * NY) + lax.axis_index("op")).astype(jnp.int32)
    dev = jnp.full((1,), dev, jnp.int32)

    b_y = [sector_bases] + [shift_y(sector_bases, d) for d in DIST]
    w_z = spread_z(wavefunction)
    b_y = jnp.stack(b_y)
    b_y, w_z = lax.optimization_barrier((b_y, w_z))
    ws = [w_z] + [shift_y(w_z, d) for d in DIST]
    b_z = spread_z(b_y)
    targets = [pair_target] + [shift_y(pair_target, d) for d in DIST]

    parts = products(dev, pair_source, sector_slot, orders, ws, left_env, right_env)
    got = [parts[0]] + [shift_y(parts[1 + k], d) for k, d in enumerate(DIST)]

    owned = join(dev, b_z)
    tables = [owned] + [shift_x(owned, d) for d in DIST]
    tables = tables + [swap_core(t) for t in tables]
    halves = half(dev, pair_source, sector_slot, owned, left_env)

    mine, other = by_target(dev, sector_slot, targets, got)
    other = swap_core(other)
    e = over_cores(dev, mine, other)
    e = [e[0]] + [shift_x(e[1 + k], d) for k, d in enumerate(DIST)]
    summed = exchange_z(over_x(e))
    sigma_blocks = over_z(dev, sector_slot, orders, summed)

    left_rotated = rotate(dev, pair_target, sector_slot, halves, tables)
    return sigma_blocks, left_rotated


def solution(mesh):
    placed = (
        P("sector", "op", None),
        P("sector", "op", None),
        P(("sector", "op"), None, None),
        P(("sector", "op"), None, None),
        P(("sector", "op")),
        P(("sector", "op")),
        P(),
        P(),
    )
    return jax.shard_map(
        per_device,
        mesh=mesh,
        in_specs=placed,
        out_specs=(P("sector", "op", None), P(("sector", "op"), None, None)),
        check_vma=False,
    )
```

```python
import jax
import jax.numpy as jnp
from jax import lax
from jax.experimental import pallas as pl
from jax.experimental.pallas import tpu as pltpu
from jax.sharding import PartitionSpec as P


NX, NC, NZ, NY = 4, 2, 8, 4
SLOTS = 2
SECTORS = 16
PAIRS = 6
ROWS = 16
K = 512
BF = jnp.bfloat16
F32 = jnp.float32
DIST = (1, 3, 2)


SMEM = pl.BlockSpec(memory_space=pltpu.SMEM)
ANY = pl.BlockSpec(memory_space=pl.ANY)


def shift_y(a, d):
    perm = [(z * NY + y, z * NY + (y + d) % NY) for z in range(NZ) for y in range(NY)]
    return lax.ppermute(a, "op", perm)


def shift_x(a, d):
    perm = [(x * NC + c, (x + d) % NX * NC + c) for x in range(NX) for c in range(NC)]
    return lax.ppermute(a, "sector", perm)


def swap_core(a):
    perm = [(x * NC + c, x * NC + 1 - c) for x in range(NX) for c in range(NC)]
    return lax.ppermute(a, "sector", perm)


def exchange_z(tiles):
    groups = [[z * NY + y for z in range(NZ)] for y in range(NY)]
    return lax.all_to_all(tiles, "op", 0, 0, axis_index_groups=groups, tiled=True)


def place(dev_ref):
    dev = dev_ref[0]
    x = dev // 64
    c = dev // 32 % 2
    z = dev // 4 % 8
    y = dev % 4
    return x, c, z, y


def order_of(slot, sector_slot, orders):
    found = jnp.int32(0)
    for s in range(SECTORS):
        found = jnp.where(sector_slot[s] == slot, orders[s], found)
    return found


def source_y(y, k):
    return y if k == 0 else (y + NY - DIST[k - 1]) % NY


def far_kernel(
    dev, pair_source, sector_slot, orders, w0, w1, w2, w3, left, right, out, wm
):
    p = pl.program_id(0)
    x, c, _, y = place(dev)
    sector = x * NC + c

    @pl.when(p == 0)
    def _():
        row_in = lax.broadcasted_iota(jnp.int32, (ROWS, K), 0)
        column = lax.broadcasted_iota(jnp.int32, (ROWS, K), 1)
        for a in range(SLOTS):
            order = order_of(sector * SLOTS + a, sector_slot, orders)
            for k, w in enumerate((w0, w1, w2, w3)):
                ys = source_y(y, k)
                for zz in range(NZ):
                    limit = order - (zz * NY + ys) * ROWS
                    keep = (row_in < limit) & (column < order)
                    value = w[zz, a].astype(F32)
                    wm[a, zz, ys] = jnp.where(keep, value, 0.0).astype(BF)

    a = sector_slot[pair_source[p]] - sector * SLOTS
    out[0] = chunk_product(left[0, :, 0].reshape(-1, K), wm[a], right[0]).reshape(NZ, ROWS, K)


def chunk_product(rows, w, right):
    projected = jnp.dot(rows, w.reshape(K, K), preferred_element_type=F32).astype(BF)
    return lax.dot_general(
        projected, right, (((1,), (1,)), ((), ())), preferred_element_type=F32
    ).astype(BF)


def near_kernel(dev, pair_source, sector_slot, wm, left, right, o0, o1, o3):
    p = pl.program_id(0)
    x, c, _, y = place(dev)
    a = sector_slot[pair_source[p]] - (x * NC + c) * SLOTS
    steps = (0,) + DIST[:2]
    rows = jnp.concatenate([left[0, :, (y + d) % NY].reshape(-1, K) for d in steps], axis=0)
    product = chunk_product(rows, wm[a], right[0])
    part = NZ * ROWS
    for k, out in enumerate((o0, o1, o3)):
        out[0] = product[k * part : (k + 1) * part].reshape(NZ, ROWS, K)


PAIR = pl.BlockSpec((1, K, K), lambda p, *_: (p, 0, 0))
PAIR_OUT = pl.BlockSpec((1, NZ, ROWS, K), lambda p, *_: (p, 0, 0, 0))
SLOT_WHOLE = pl.BlockSpec((SLOTS, NZ, NY, ROWS, K), lambda p, *_: (0, 0, 0, 0, 0))
CHUNK = jax.ShapeDtypeStruct((PAIRS, NZ, ROWS, K), BF)


def far_products(dev, pair_source, sector_slot, orders, ws, left, right):
    whole = pl.BlockSpec((NZ, SLOTS, ROWS, K), lambda p, *_: (0, 0, 0, 0))
    rows = pl.BlockSpec(
        (1, NZ, 1, ROWS, K), lambda p, dev, *_: (p, 0, (dev[0] % NY + DIST[2]) % NY, 0, 0)
    )
    return pl.pallas_call(
        far_kernel,
        out_shape=[CHUNK, jax.ShapeDtypeStruct((SLOTS, NZ, NY, ROWS, K), BF)],
        grid_spec=pltpu.PrefetchScalarGridSpec(
            num_scalar_prefetch=4,
            grid=(PAIRS,),
            in_specs=[whole] * 4 + [rows, PAIR],
            out_specs=[PAIR_OUT, SLOT_WHOLE],
        ),
        name="far_products",
    )(dev, pair_source, sector_slot, orders, *ws, left, right)


def near_products(dev, pair_source, sector_slot, wm, left, right):
    return pl.pallas_call(
        near_kernel,
        out_shape=[CHUNK] * 3,
        grid_spec=pltpu.PrefetchScalarGridSpec(
            num_scalar_prefetch=3,
            grid=(PAIRS,),
            in_specs=[
                SLOT_WHOLE,
                pl.BlockSpec((1, NZ, NY, ROWS, K), lambda p, *_: (p, 0, 0, 0, 0)),
                PAIR,
            ],
            out_specs=[PAIR_OUT] * 3,
        ),
        name="near_products",
    )(dev, pair_source, sector_slot, wm, left, right)


def half_kernel(dev, pair_source, sector_slot, basis0, basis1, left, out, ordered):
    p = pl.program_id(0)
    x, c, _, y = place(dev)

    @pl.when(p == 0)
    def _():
        for k in range(NY):
            ordered[0, :, source_y(y, k)] = basis0[:, k]
            ordered[1, :, source_y(y, k)] = basis1[:, 0, k]

    a = sector_slot[pair_source[p]] - (x * NC + c) * SLOTS
    out[0] = jnp.dot(left[0], ordered[a].reshape(K, K), preferred_element_type=F32).astype(BF)


def half(dev, pair_source, sector_slot, basis0, basis1, left):
    pair = pl.BlockSpec((1, K, K), lambda p: (p, 0, 0))
    return pl.pallas_call(
        half_kernel,
        grid=(PAIRS,),
        out_shape=jax.ShapeDtypeStruct((PAIRS, K, K), BF),
        in_specs=[SMEM] * 3
        + [
            pl.BlockSpec((NZ, NY, ROWS, K), lambda p: (0, 0, 0, 0)),
            pl.BlockSpec((NZ, 1, NY, ROWS, K), lambda p: (0, 0, 0, 0, 0)),
            pair,
        ],
        out_specs=pair,
        scratch_shapes=[pltpu.VMEM((SLOTS, NZ, NY, ROWS, K), BF)],
        name="half",
    )(dev, pair_source, sector_slot, basis0, basis1, left)


def rotate_kernel(dev, pair_target, sector_slot, half_ref, *rest):
    tables, out, chosen, sems = rest[:10], rest[10], rest[11], rest[12]
    p = pl.program_id(0)
    x, c, _, y = place(dev)

    @pl.when(p == 0)
    def _():
        def fetch(q, carry):
            slot = sector_slot[pair_target[q]]
            sector = slot // SLOTS
            a = slot % SLOTS
            behind = (x + NX - sector // NC) % NX
            at = jnp.where(behind == 3, 2, jnp.where(behind == 2, 3, behind))
            other = (sector % NC + c) % 2

            def copy(source, k):
                pltpu.make_async_copy(
                    source, chosen.at[q, :, source_y(y, k)], sems.at[q]
                ).start()

            for core in range(NC):
                mine = tables[core * 5 : core * 5 + 5]
                for n in range(NX):

                    @pl.when((other == core) & (a == 0) & (at == n))
                    def _(table=mine[n]):
                        for k in range(NY):
                            copy(table.at[:, k], k)

                @pl.when((other == core) & (a == 1))
                def _(table=mine[4]):
                    for k in range(NY):
                        copy(table.at[:, at, k], k)

            return carry

        lax.fori_loop(0, PAIRS, fetch, 0)

    pltpu.make_async_copy(chosen.at[p], chosen.at[p], sems.at[p]).wait()
    basis = chosen[p].reshape(K, K)
    out[0] = lax.dot_general(
        basis, half_ref[0], (((0,), (0,)), ((), ())), preferred_element_type=F32
    ).astype(BF)


def rotate(dev, pair_target, sector_slot, halves, tables):
    pair = pl.BlockSpec((1, K, K), lambda p: (p, 0, 0))
    return pl.pallas_call(
        rotate_kernel,
        grid=(PAIRS,),
        out_shape=jax.ShapeDtypeStruct((PAIRS, K, K), BF),
        in_specs=[SMEM] * 3 + [pair] + [ANY] * 10,
        out_specs=pair,
        scratch_shapes=[
            pltpu.VMEM((PAIRS, NZ, NY, ROWS, K), BF),
            pltpu.SemaphoreType.DMA((PAIRS,)),
        ],
        name="rotate",
    )(dev, pair_target, sector_slot, halves, *tables)


ZB = 2


def by_target_kernel(dev, sector_slot, t0, t1, t2, t3, g0, g1, g2, g3, mine, other, acc):
    _, c, _, _ = place(dev)
    acc[...] = jnp.zeros_like(acc)
    for t, g in zip((t0, t1, t2, t3), (g0, g1, g2, g3)):
        for p in range(PAIRS):
            slot = sector_slot[t[p]]
            acc[slot] += g[p].astype(F32)
    for j in range(8):
        base = j // 2 * 4 + j % 2
        mine[j] = acc[base + c * 2]
        other[j] = acc[base + (1 - c) * 2].astype(BF)


def by_target(dev, sector_slot, targets, gathered):
    got = pl.BlockSpec((PAIRS, ZB, ROWS, K), lambda z: (0, z, 0, 0))
    out = pl.BlockSpec((8, ZB, ROWS, K), lambda z: (0, z, 0, 0))
    return pl.pallas_call(
        by_target_kernel,
        grid=(NZ // ZB,),
        out_shape=[
            jax.ShapeDtypeStruct((8, NZ, ROWS, K), F32),
            jax.ShapeDtypeStruct((8, NZ, ROWS, K), BF),
        ],
        in_specs=[SMEM] * 6 + [got] * 4,
        out_specs=[out] * 2,
        scratch_shapes=[pltpu.VMEM((SECTORS, ZB, ROWS, K), F32)],
        name="by_target",
    )(dev, sector_slot, *targets, *gathered)


def over_cores_kernel(dev, mine, other, e0, e1, e2, e3):
    x, _, _, _ = place(dev)
    for d, out in zip((0,) + DIST, (e0, e1, e2, e3)):
        xd = (x + d) % NX
        for a in range(SLOTS):
            j = xd * SLOTS + a
            out[a] = (mine[j] + other[j].astype(F32)).astype(out.dtype)


def over_cores(dev, mine, other):
    zb = 4
    got = pl.BlockSpec((8, zb, ROWS, K), lambda z: (0, z, 0, 0))
    out = pl.BlockSpec((SLOTS, zb, ROWS, K), lambda z: (0, z, 0, 0))
    shape = (SLOTS, NZ, ROWS, K)
    return pl.pallas_call(
        over_cores_kernel,
        grid=(NZ // zb,),
        out_shape=[jax.ShapeDtypeStruct(shape, F32)] + [jax.ShapeDtypeStruct(shape, BF)] * 3,
        in_specs=[SMEM] + [got] * 2,
        out_specs=[out] * 4,
        name="over_cores",
    )(dev, mine, other)


def over_x_kernel(e0, e1, e2, e3, out):
    for a in range(SLOTS):
        total = e0[a] + e1[a].astype(F32) + e2[a].astype(F32) + e3[a].astype(F32)
        out[:, a] = total.astype(BF)


def over_x(parts):
    vm = pl.BlockSpec(memory_space=pltpu.VMEM)
    return pl.pallas_call(
        over_x_kernel,
        out_shape=jax.ShapeDtypeStruct((NZ, SLOTS, ROWS, K), BF),
        in_specs=[vm] * 4,
        out_specs=vm,
        name="over_x",
    )(*parts)


def over_z_kernel(dev, sector_slot, orders, parts, out):
    x, c, z, y = place(dev)
    row = lax.broadcasted_iota(jnp.int32, (ROWS, K), 0) + (z * NY + y) * ROWS
    column = lax.broadcasted_iota(jnp.int32, (ROWS, K), 1)
    for a in range(SLOTS):
        order = order_of((x * NC + c) * SLOTS + a, sector_slot, orders)
        total = parts[0, a].astype(F32)
        for k in range(1, NZ):
            total = total + parts[k, a].astype(F32)
        keep = (row < order) & (column < order)
        out[a] = jnp.where(keep, total, 0.0).astype(BF)


def over_z(dev, sector_slot, orders, parts):
    vm = pl.BlockSpec(memory_space=pltpu.VMEM)
    return pl.pallas_call(
        over_z_kernel,
        out_shape=jax.ShapeDtypeStruct((SLOTS, ROWS, K), BF),
        in_specs=[SMEM] * 3 + [vm],
        out_specs=vm,
        name="over_z",
    )(dev, sector_slot, orders, parts)


def spread_z(a):
    return exchange_z(jnp.broadcast_to(a, (NZ, *a.shape)))


def per_device(
    wavefunction, sector_bases, left_env, right_env, pair_source, pair_target, sector_slot, orders
):
    dev = (lax.axis_index("sector") * (NZ * NY) + lax.axis_index("op")).astype(jnp.int32)
    dev = jnp.full((1,), dev, jnp.int32)

    w_z = spread_z(wavefunction)
    b_y = [sector_bases] + [shift_y(sector_bases, d) for d in DIST]
    b_y = jnp.stack(b_y)
    b_y, w_z = lax.optimization_barrier((b_y, w_z))
    ws = [w_z] + [shift_y(w_z, d) for d in DIST]
    b_0 = spread_z(b_y[:, 0])
    b_1 = b_y[:, 1]
    b_1 = jnp.stack([b_1] + [shift_x(b_1, d) for d in DIST])
    b_1 = spread_z(b_1)
    targets = [pair_target] + [shift_y(pair_target, d) for d in DIST]

    left = left_env.reshape(PAIRS, NZ, NY, ROWS, K)
    far, wm = far_products(dev, pair_source, sector_slot, orders, ws, left, right_env)
    far = shift_y(far, 2)
    near = near_products(dev, pair_source, sector_slot, wm, left, right_env)
    got = [near[0], shift_y(near[1], 1), shift_y(near[2], 3), far]

    tables = [b_0] + [shift_x(b_0, d) for d in DIST] + [b_1]
    tables = tables + [swap_core(t) for t in tables]
    halves = half(dev, pair_source, sector_slot, b_0, b_1, left_env)

    mine, other = by_target(dev, sector_slot, targets, got)
    other = swap_core(other)
    e = over_cores(dev, mine, other)
    e = [e[0]] + [shift_x(e[1 + k], d) for k, d in enumerate(DIST)]
    summed = exchange_z(over_x(e))
    sigma_blocks = over_z(dev, sector_slot, orders, summed)

    left_rotated = rotate(dev, pair_target, sector_slot, halves, tables)
    return sigma_blocks, left_rotated


def solution(mesh):
    placed = (
        P("sector", "op", None),
        P("sector", "op", None),
        P(("sector", "op"), None, None),
        P(("sector", "op"), None, None),
        P(("sector", "op")),
        P(("sector", "op")),
        P(),
        P(),
    )
    return jax.shard_map(
        per_device,
        mesh=mesh,
        in_specs=placed,
        out_specs=(P("sector", "op", None), P(("sector", "op"), None, None)),
        check_vma=False,
    )
```

```python
import jax
import jax.numpy as jnp
from jax import lax
from jax.experimental import pallas as pl
from jax.experimental.pallas import tpu as pltpu
from jax.sharding import PartitionSpec as P


NX, NC, NZ, NY = 4, 2, 8, 4
SLOTS = 2
SECTORS = 16
PAIRS = 6
ROWS = 16
K = 512
BF = jnp.bfloat16
F32 = jnp.float32
DIST = (1, 3, 2)


SMEM = pl.BlockSpec(memory_space=pltpu.SMEM)
ANY = pl.BlockSpec(memory_space=pl.ANY)


def shift_y(a, d):
    perm = [(z * NY + y, z * NY + (y + d) % NY) for z in range(NZ) for y in range(NY)]
    return lax.ppermute(a, "op", perm)


def shift_x(a, d):
    perm = [(x * NC + c, (x + d) % NX * NC + c) for x in range(NX) for c in range(NC)]
    return lax.ppermute(a, "sector", perm)


def swap_core(a):
    perm = [(x * NC + c, x * NC + 1 - c) for x in range(NX) for c in range(NC)]
    return lax.ppermute(a, "sector", perm)


def exchange_z(tiles):
    groups = [[z * NY + y for z in range(NZ)] for y in range(NY)]
    return lax.all_to_all(tiles, "op", 0, 0, axis_index_groups=groups, tiled=True)


def place(dev_ref):
    dev = dev_ref[0]
    x = dev // 64
    c = dev // 32 % 2
    z = dev // 4 % 8
    y = dev % 4
    return x, c, z, y


def order_of(slot, sector_slot, orders):
    found = jnp.int32(0)
    for s in range(SECTORS):
        found = jnp.where(sector_slot[s] == slot, orders[s], found)
    return found


def source_y(y, k):
    return y if k == 0 else (y + NY - DIST[k - 1]) % NY


def far_kernel(
    dev, pair_source, sector_slot, orders, w0, w1, w2, w3, left, right, out, wm
):
    p = pl.program_id(0)
    x, c, _, y = place(dev)
    sector = x * NC + c

    @pl.when(p == 0)
    def _():
        row_in = lax.broadcasted_iota(jnp.int32, (ROWS, K), 0)
        column = lax.broadcasted_iota(jnp.int32, (ROWS, K), 1)
        for a in range(SLOTS):
            order = order_of(sector * SLOTS + a, sector_slot, orders)
            for k, w in enumerate((w0, w1, w2, w3)):
                ys = source_y(y, k)
                for zz in range(NZ):
                    limit = order - (zz * NY + ys) * ROWS
                    keep = (row_in < limit) & (column < order)
                    value = w[zz, a].astype(F32)
                    wm[a, zz, ys] = jnp.where(keep, value, 0.0).astype(BF)

    a = sector_slot[pair_source[p]] - sector * SLOTS
    out[0] = chunk_product(left[0, :, 0].reshape(-1, K), wm[a], right[0]).reshape(NZ, ROWS, K)


def chunk_product(rows, w, right):
    projected = jnp.dot(rows, w.reshape(K, K), preferred_element_type=F32).astype(BF)
    return lax.dot_general(
        projected, right, (((1,), (1,)), ((), ())), preferred_element_type=F32
    ).astype(BF)


def near_kernel(dev, pair_source, sector_slot, wm, left, right, o0, o1, o3):
    p = pl.program_id(0)
    x, c, _, y = place(dev)
    a = sector_slot[pair_source[p]] - (x * NC + c) * SLOTS
    steps = (0,) + DIST[:2]
    rows = jnp.concatenate([left[0, :, (y + d) % NY].reshape(-1, K) for d in steps], axis=0)
    product = chunk_product(rows, wm[a], right[0])
    part = NZ * ROWS
    for k, out in enumerate((o0, o1, o3)):
        out[0] = product[k * part : (k + 1) * part].reshape(NZ, ROWS, K)


PAIR = pl.BlockSpec((1, K, K), lambda p, *_: (p, 0, 0))
PAIR_OUT = pl.BlockSpec((1, NZ, ROWS, K), lambda p, *_: (p, 0, 0, 0))
SLOT_WHOLE = pl.BlockSpec((SLOTS, NZ, NY, ROWS, K), lambda p, *_: (0, 0, 0, 0, 0))
CHUNK = jax.ShapeDtypeStruct((PAIRS, NZ, ROWS, K), BF)


def far_products(dev, pair_source, sector_slot, orders, ws, left, right):
    whole = pl.BlockSpec((NZ, SLOTS, ROWS, K), lambda p, *_: (0, 0, 0, 0))
    rows = pl.BlockSpec(
        (1, NZ, 1, ROWS, K), lambda p, dev, *_: (p, 0, (dev[0] % NY + DIST[2]) % NY, 0, 0)
    )
    return pl.pallas_call(
        far_kernel,
        out_shape=[CHUNK, jax.ShapeDtypeStruct((SLOTS, NZ, NY, ROWS, K), BF)],
        grid_spec=pltpu.PrefetchScalarGridSpec(
            num_scalar_prefetch=4,
            grid=(PAIRS,),
            in_specs=[whole] * 4 + [rows, PAIR],
            out_specs=[PAIR_OUT, SLOT_WHOLE],
        ),
        name="far_products",
    )(dev, pair_source, sector_slot, orders, *ws, left, right)


def near_products(dev, pair_source, sector_slot, wm, left, right):
    return pl.pallas_call(
        near_kernel,
        out_shape=[CHUNK] * 3,
        grid_spec=pltpu.PrefetchScalarGridSpec(
            num_scalar_prefetch=3,
            grid=(PAIRS,),
            in_specs=[
                SLOT_WHOLE,
                pl.BlockSpec((1, NZ, NY, ROWS, K), lambda p, *_: (p, 0, 0, 0, 0)),
                PAIR,
            ],
            out_specs=[PAIR_OUT] * 3,
        ),
        name="near_products",
    )(dev, pair_source, sector_slot, wm, left, right)


def half_kernel(dev, pair_source, sector_slot, bases, left, out, ordered):
    p = pl.program_id(0)
    x, c, _, y = place(dev)

    @pl.when(p == 0)
    def _():
        for k in range(NY):
            for a in range(SLOTS):
                ordered[a, :, source_y(y, k)] = bases[:, a, k]

    a = sector_slot[pair_source[p]] - (x * NC + c) * SLOTS
    out[0] = jnp.dot(left[0], ordered[a].reshape(K, K), preferred_element_type=F32).astype(BF)


def half(dev, pair_source, sector_slot, bases, left):
    pair = pl.BlockSpec((1, K, K), lambda p: (p, 0, 0))
    return pl.pallas_call(
        half_kernel,
        grid=(PAIRS,),
        out_shape=jax.ShapeDtypeStruct((PAIRS, K, K), BF),
        in_specs=[SMEM] * 3
        + [
            pl.BlockSpec((NZ, SLOTS, NY, ROWS, K), lambda p: (0, 0, 0, 0, 0)),
            pair,
        ],
        out_specs=pair,
        scratch_shapes=[pltpu.VMEM((SLOTS, NZ, NY, ROWS, K), BF)],
        name="half",
    )(dev, pair_source, sector_slot, bases, left)


def rotate_kernel(dev, pair_target, sector_slot, half_ref, *rest):
    tables, out, chosen, sems = rest[:10], rest[10], rest[11], rest[12]
    p = pl.program_id(0)
    x, c, _, y = place(dev)

    @pl.when(p == 0)
    def _():
        def fetch(q, carry):
            slot = sector_slot[pair_target[q]]
            sector = slot // SLOTS
            a = slot % SLOTS
            behind = (x + NX - sector // NC) % NX
            at = jnp.where(behind == 3, 2, jnp.where(behind == 2, 3, behind))
            other = (sector % NC + c) % 2

            def copy(source, k):
                pltpu.make_async_copy(
                    source, chosen.at[q, :, source_y(y, k)], sems.at[q]
                ).start()

            for core in range(NC):
                mine = tables[core * 5 : core * 5 + 5]

                @pl.when((other == core) & (at == 0))
                def _(table=mine[0]):
                    for k in range(NY):
                        copy(table.at[:, a, k], k)

                for n in range(1, NX):

                    @pl.when((other == core) & (a == 0) & (at == n))
                    def _(table=mine[n]):
                        for k in range(NY):
                            copy(table.at[:, k], k)

                @pl.when((other == core) & (a == 1) & (at > 0))
                def _(table=mine[4]):
                    for k in range(NY):
                        copy(table.at[:, at - 1, k], k)

            return carry

        lax.fori_loop(0, PAIRS, fetch, 0)

    pltpu.make_async_copy(chosen.at[p], chosen.at[p], sems.at[p]).wait()
    basis = chosen[p].reshape(K, K)
    out[0] = lax.dot_general(
        basis, half_ref[0], (((0,), (0,)), ((), ())), preferred_element_type=F32
    ).astype(BF)


def rotate(dev, pair_target, sector_slot, halves, tables):
    pair = pl.BlockSpec((1, K, K), lambda p: (p, 0, 0))
    return pl.pallas_call(
        rotate_kernel,
        grid=(PAIRS,),
        out_shape=jax.ShapeDtypeStruct((PAIRS, K, K), BF),
        in_specs=[SMEM] * 3 + [pair] + [ANY] * 10,
        out_specs=pair,
        scratch_shapes=[
            pltpu.VMEM((PAIRS, NZ, NY, ROWS, K), BF),
            pltpu.SemaphoreType.DMA((PAIRS,)),
        ],
        name="rotate",
    )(dev, pair_target, sector_slot, halves, *tables)


ZB = 2


def by_target_kernel(dev, sector_slot, t0, t1, t2, t3, g0, g1, g2, g3, mine, other, acc):
    _, c, _, _ = place(dev)
    acc[...] = jnp.zeros_like(acc)
    for t, g in zip((t0, t1, t2, t3), (g0, g1, g2, g3)):
        for p in range(PAIRS):
            slot = sector_slot[t[p]]
            acc[slot] += g[p].astype(F32)
    for j in range(8):
        base = j // 2 * 4 + j % 2
        mine[j] = acc[base + c * 2]
        other[j] = acc[base + (1 - c) * 2].astype(BF)


def by_target(dev, sector_slot, targets, gathered):
    got = pl.BlockSpec((PAIRS, ZB, ROWS, K), lambda z: (0, z, 0, 0))
    out = pl.BlockSpec((8, ZB, ROWS, K), lambda z: (0, z, 0, 0))
    return pl.pallas_call(
        by_target_kernel,
        grid=(NZ // ZB,),
        out_shape=[
            jax.ShapeDtypeStruct((8, NZ, ROWS, K), F32),
            jax.ShapeDtypeStruct((8, NZ, ROWS, K), BF),
        ],
        in_specs=[SMEM] * 6 + [got] * 4,
        out_specs=[out] * 2,
        scratch_shapes=[pltpu.VMEM((SECTORS, ZB, ROWS, K), F32)],
        name="by_target",
    )(dev, sector_slot, *targets, *gathered)


def over_cores_kernel(dev, mine, other, e0, e1, e2, e3):
    x, _, _, _ = place(dev)
    for d, out in zip((0,) + DIST, (e0, e1, e2, e3)):
        xd = (x + d) % NX
        for a in range(SLOTS):
            j = xd * SLOTS + a
            out[a] = (mine[j] + other[j].astype(F32)).astype(out.dtype)


def over_cores(dev, mine, other):
    zb = 4
    got = pl.BlockSpec((8, zb, ROWS, K), lambda z: (0, z, 0, 0))
    out = pl.BlockSpec((SLOTS, zb, ROWS, K), lambda z: (0, z, 0, 0))
    shape = (SLOTS, NZ, ROWS, K)
    return pl.pallas_call(
        over_cores_kernel,
        grid=(NZ // zb,),
        out_shape=[jax.ShapeDtypeStruct(shape, F32)] + [jax.ShapeDtypeStruct(shape, BF)] * 3,
        in_specs=[SMEM] + [got] * 2,
        out_specs=[out] * 4,
        name="over_cores",
    )(dev, mine, other)


def over_x_kernel(e0, e1, e2, e3, out):
    for a in range(SLOTS):
        total = e0[a] + e1[a].astype(F32) + e2[a].astype(F32) + e3[a].astype(F32)
        out[:, a] = total.astype(BF)


def over_x(parts):
    vm = pl.BlockSpec(memory_space=pltpu.VMEM)
    return pl.pallas_call(
        over_x_kernel,
        out_shape=jax.ShapeDtypeStruct((NZ, SLOTS, ROWS, K), BF),
        in_specs=[vm] * 4,
        out_specs=vm,
        name="over_x",
    )(*parts)


def over_z_kernel(dev, sector_slot, orders, parts, out):
    x, c, z, y = place(dev)
    row = lax.broadcasted_iota(jnp.int32, (ROWS, K), 0) + (z * NY + y) * ROWS
    column = lax.broadcasted_iota(jnp.int32, (ROWS, K), 1)
    for a in range(SLOTS):
        order = order_of((x * NC + c) * SLOTS + a, sector_slot, orders)
        total = parts[0, a].astype(F32)
        for k in range(1, NZ):
            total = total + parts[k, a].astype(F32)
        keep = (row < order) & (column < order)
        out[a] = jnp.where(keep, total, 0.0).astype(BF)


def over_z(dev, sector_slot, orders, parts):
    vm = pl.BlockSpec(memory_space=pltpu.VMEM)
    return pl.pallas_call(
        over_z_kernel,
        out_shape=jax.ShapeDtypeStruct((SLOTS, ROWS, K), BF),
        in_specs=[SMEM] * 3 + [vm],
        out_specs=vm,
        name="over_z",
    )(dev, sector_slot, orders, parts)


def spread_z(a):
    return exchange_z(jnp.broadcast_to(a, (NZ, *a.shape)))


def per_device(
    wavefunction, sector_bases, left_env, right_env, pair_source, pair_target, sector_slot, orders
):
    dev = (lax.axis_index("sector") * (NZ * NY) + lax.axis_index("op")).astype(jnp.int32)
    dev = jnp.full((1,), dev, jnp.int32)

    w_z = spread_z(wavefunction)
    b_y = [sector_bases] + [shift_y(sector_bases, d) for d in DIST]
    b_y = jnp.stack(b_y, axis=1)
    b_y, w_z = lax.optimization_barrier((b_y, w_z))
    ws = [w_z] + [shift_y(w_z, d) for d in DIST]
    b_0 = spread_z(b_y)
    b_1 = jnp.stack([shift_x(b_y[1], d) for d in DIST])
    b_1 = spread_z(b_1)
    targets = [pair_target] + [shift_y(pair_target, d) for d in DIST]

    left = left_env.reshape(PAIRS, NZ, NY, ROWS, K)
    far, wm = far_products(dev, pair_source, sector_slot, orders, ws, left, right_env)
    far = shift_y(far, 2)
    near = near_products(dev, pair_source, sector_slot, wm, left, right_env)
    got = [near[0], shift_y(near[1], 1), shift_y(near[2], 3), far]

    slot_0 = b_0[:, 0]
    tables = [b_0] + [shift_x(slot_0, d) for d in DIST] + [b_1]
    tables = tables + [swap_core(t) for t in tables]
    halves = half(dev, pair_source, sector_slot, b_0, left_env)

    mine, other = by_target(dev, sector_slot, targets, got)
    other = swap_core(other)
    e = over_cores(dev, mine, other)
    e = [e[0]] + [shift_x(e[1 + k], d) for k, d in enumerate(DIST)]
    summed = exchange_z(over_x(e))
    sigma_blocks = over_z(dev, sector_slot, orders, summed)

    left_rotated = rotate(dev, pair_target, sector_slot, halves, tables)
    return sigma_blocks, left_rotated


def solution(mesh):
    placed = (
        P("sector", "op", None),
        P("sector", "op", None),
        P(("sector", "op"), None, None),
        P(("sector", "op"), None, None),
        P(("sector", "op")),
        P(("sector", "op")),
        P(),
        P(),
    )
    return jax.shard_map(
        per_device,
        mesh=mesh,
        in_specs=placed,
        out_specs=(P("sector", "op", None), P(("sector", "op"), None, None)),
        check_vma=False,
    )
```
